32 devices in a mesh: section: 2 (over core), shard: 4 (over y, x), replica: 4 (over z).
Axes of the slice: x: 2, y: 2, z: 4, core: 2. Of those that a mesh axis runs over, the one named last changes fastest.
Arguments:
- block_input: bfloat16 [32, 256, 1152], P(('shard', 'replica')), may hold values from -16 to 16
- labels: int32 [32], P(('shard', 'replica')), may hold values from 0 to 1000
- timesteps: int32 [32], P(('shard', 'replica')), may hold values from 0 to 999
- label_table: bfloat16 [1001, 1152], replicated, may hold values from -5 to 5
- time_table: bfloat16 [1000, 1152], replicated, may hold values from -5 to 5
- ada_weight: bfloat16 [2, 1152, 6912], P('section', 'shard'), may hold values from -0.1875 to 0.1875
- qkv_weight: bfloat16 [2, 1152, 3456], P('section', 'shard'), may hold values from -0.1875 to 0.1875
- proj_weight: bfloat16 [2, 1152, 1152], P('section', 'shard'), may hold values from -0.75 to 0.75
- fc1_weight: bfloat16 [2, 1152, 4608], P('section', 'shard'), may hold values from -0.1875 to 0.1875
- fc2_weight: bfloat16 [2, 4608, 1152], P('section', 'shard'), may hold values from -0.09375 to 0.09375
- block_bias: bfloat16 [2, 16128], P('section', 'shard'), may hold values from -3 to 3
- output_cotangent: bfloat16 [32, 256, 1152], P(('shard', 'replica')), may hold values from -6 to 6
Outputs:
- block_outputs: bfloat16 [2, 32, 256, 1152], P('section', ('shard', 'replica'))
- input_grads: bfloat16 [2, 32, 256, 1152], P('section', ('shard', 'replica'))
- ada_grad: float32 [2, 1152, 6912], P('section', 'shard')
- qkv_grad: float32 [2, 1152, 3456], P('section', 'shard')
- proj_grad: float32 [2, 1152, 1152], P('section', 'shard')
- fc1_grad: float32 [2, 1152, 4608], P('section', 'shard')
- fc2_grad: float32 [2, 4608, 1152], P('section', 'shard')
- bias_grad: float32 [2, 16128], P('section', 'shard')
- label_table_grad: float32 [1001, 1152], replicated
- time_table_grad: float32 [1000, 1152], replicated
The draws below stay inside these ranges and needn't reach their ends.
All inputs are finite; a program needn't handle non-finite values.
Results may differ from the reference program's by a relative error of at most 0.035.
Values may be sent and summed in bfloat16 or wider, within the bound.
No kernel may reach another device: no remote copies, remote signals or barrier semaphores. Data moves between devices by JAX's collectives and lax.ppermute only.
A program may use at most 384 MiB of HBM per device.

```python
import jax
import jax.numpy as jnp
from jax import lax

D = 1152
HEADS = 16
HEAD_DIM = 72
FF = 4608
CLASSES = 1001
TSTEPS = 1000
LEN = 256
LATENTS = 32
BIAS_LEN = 16128


def draw_block_input(key, part):
    key_noise, key_rows, key_cols = jax.random.split(key, 3)
    row_scale = jnp.exp(jax.random.uniform(key_rows, (LATENTS, LEN, 1), jnp.float32, -1.15, 1.15))
    col_scale = jnp.exp(jax.random.uniform(key_cols, (1, 1, D), jnp.float32, -1.15, 1.15))
    noise = jax.random.normal(key_noise, (LATENTS, LEN, D), jnp.float32)
    values_out = noise * row_scale * col_scale
    return jnp.clip(values_out, -16.0, 16.0).astype(jnp.bfloat16)


def touch_ends(entries, own_key, least, high):
    longest = entries.shape.index(max(entries.shape))
    spots = []
    for shift in (0, 1):
        where = [jax.random.randint(jax.random.fold_in(own_key, axis), (), 0, length) for axis, length in enumerate(entries.shape)]
        where[longest] = (where[longest] + shift) % entries.shape[longest]
        spots.append(tuple(where))
    return entries.at[spots[0]].set(least).at[spots[1]].set(high)


def shard_levels(own_key, dims, cuts, smallest, largest):
    level, own = 1.0, jax.random.fold_in(own_key, 6)
    for axis_at, blocks in cuts:
        draws = jnp.exp(jax.random.uniform(jax.random.fold_in(own, axis_at), (blocks,), jnp.float32, smallest / len(cuts), largest / len(cuts)))
        level = level * jnp.repeat(draws, dims[axis_at] // blocks).reshape([-1 if axis == axis_at else 1 for axis in range(len(dims))])
    return level


def bell_draw(own_key, dims, width, limit, cuts=(), dtype=jnp.bfloat16):
    result = jax.random.normal(own_key, dims, jnp.float32) * width
    if len(cuts) > 0:
        result = shard_levels(own_key, dims, cuts, -0.22, 0.18) * result
    return jnp.clip(result, min=-limit, max=limit).astype(dtype)


def setup_inputs(seed: int = 0) -> dict:
    arg_keys = jax.random.split(jax.random.key(seed), 13)
    return {
        "block_input": draw_block_input(jax.random.fold_in(arg_keys[12], 71), 0),
        "labels": touch_ends(jax.random.randint(arg_keys[1], (LATENTS,), 0, CLASSES), jax.random.fold_in(arg_keys[1], 1), 0, CLASSES - 1).astype(jnp.int32),
        "timesteps": touch_ends(jax.random.randint(arg_keys[2], (LATENTS,), 0, TSTEPS), jax.random.fold_in(arg_keys[2], 1), 0, TSTEPS - 1).astype(jnp.int32),
        "label_table": bell_draw(arg_keys[3], (CLASSES, D), 1.0, 5.0),
        "time_table": bell_draw(arg_keys[4], (TSTEPS, D), 1.0, 5.0),
        "ada_weight": bell_draw(arg_keys[5], (2, D, 6 * D), D ** -0.5, 0.1875, ((0, 2), (1, 4))),
        "qkv_weight": bell_draw(arg_keys[6], (2, D, 3 * D), D ** -0.5, 0.1875, ((0, 2), (1, 4))),
        "proj_weight": bell_draw(arg_keys[7], (2, D, D), (D // 16) ** -0.5, 0.75, ((0, 2), (1, 4))),
        "fc1_weight": bell_draw(arg_keys[8], (2, D, FF), D ** -0.5, 0.1875, ((0, 2), (1, 4))),
        "fc2_weight": bell_draw(arg_keys[9], (2, FF, D), FF ** -0.5, 0.09375, ((0, 2), (1, 4))),
        "block_bias": bell_draw(arg_keys[10], (2, BIAS_LEN), 0.5, 3.0, ((0, 2), (1, 4))),
        "output_cotangent": bell_draw(arg_keys[11], (LATENTS, LEN, D), 1.0, 6.0, ((0, 16),)),
    }


@jax.custom_vjp
def low(v):
    return lax.optimization_barrier(v.astype(jnp.bfloat16)).astype(jnp.float32)

@jax.custom_vjp
def low_back(v):
    return v

def low_keep(v):
    return (low(v), None)

def low_pass(kept, grad):
    return (grad,)

def back_keep(v):
    return (v, None)

def back_low(kept, grad):
    return (low(grad),)
low.defvjp(low_keep, low_pass)
low_back.defvjp(back_keep, back_low)
highest = lax.Precision.HIGHEST
layer_eps = 1e-06

def layer_norm(residual_state):
    centred = residual_state - lax.optimization_barrier(jnp.mean(residual_state, axis=-1, keepdims=True))
    return centred * lax.rsqrt(lax.optimization_barrier(jnp.mean(centred * centred, axis=-1, keepdims=True)) + layer_eps)

def attend_one(stacked):
    queries = stacked[0]
    keys_in = stacked[1]
    values_in = stacked[2]
    scores = low_back(jnp.einsum('shd,thd->hst', queries, keys_in, precision=highest) * HEAD_DIM ** (-0.5))
    attn_probs = jax.nn.softmax(scores, axis=-1)
    return low_back(jnp.einsum('hst,thd->shd', low(attn_probs), values_in, precision=highest))

def diffusion_block(residual_state, condition_activation, modulation_weight, query_key_value_weight, projection_weight, expand_weight, contract_weight, stacked_biases):
    lat_count = residual_state.shape[0]
    mod_all = low_back(jnp.dot(condition_activation, modulation_weight, precision=highest)) + stacked_biases[:6 * D]
    mod_parts = [mod_all[:, None, part_index * D:(part_index + 1) * D] for part_index in range(6)]
    shift_one, scale_one, gate_one, shift_two, scale_two, gate_two = mod_parts
    hidden_one = low(layer_norm(residual_state) * (1.0 + scale_one) + shift_one)
    qkv_bias = jnp.concatenate([stacked_biases[6 * D:7 * D], jnp.zeros_like(stacked_biases[:D]), stacked_biases[7 * D:8 * D]])
    qkv_all = low_back(jnp.einsum('lsd,de->lse', hidden_one, query_key_value_weight, precision=highest)) + qkv_bias
    head_shape = (lat_count, LEN, HEADS, HEAD_DIM)
    queries = low(qkv_all[..., :D]).reshape(head_shape)
    keys_in = low(qkv_all[..., D:2 * D]).reshape(head_shape)
    values_in = low(qkv_all[..., 2 * D:]).reshape(head_shape)
    stacked = jnp.stack([queries, keys_in, values_in], axis=1)
    attended = lax.map(jax.checkpoint(attend_one), stacked).reshape(lat_count, LEN, D)
    attn_out = low_back(jnp.einsum('lsd,de->lse', low(attended), projection_weight, precision=highest)) + stacked_biases[8 * D:9 * D]
    mixed = residual_state + gate_one * attn_out
    hidden_two = low(layer_norm(mixed) * (1.0 + scale_two) + shift_two)
    pre_act = low_back(jnp.einsum('lsd,de->lse', hidden_two, expand_weight, precision=highest)) + stacked_biases[9 * D:9 * D + FF]
    mlp_act = low(jax.nn.gelu(pre_act, approximate=True))
    mlp_out = low_back(jnp.einsum('lse,ed->lsd', mlp_act, contract_weight, precision=highest)) + stacked_biases[9 * D + FF:]
    return mixed + gate_two * mlp_out

def reference(block_input, labels, timesteps, label_table, time_table, ada_weight, qkv_weight, proj_weight, fc1_weight, fc2_weight, block_bias, output_cotangent):

    def forward(residual_state, label_tab, time_tab, probe, modulation_weight, query_key_value_weight, projection_weight, expand_weight, contract_weight, stacked_biases):
        condition = label_tab[labels] + time_tab[timesteps]
        condition_activation = low(jax.nn.silu(condition))
        leading_block = diffusion_block(residual_state, condition_activation, modulation_weight[0], query_key_value_weight[0], projection_weight[0], expand_weight[0], contract_weight[0], stacked_biases[0])
        trailing_input = low_back(low(leading_block)) + probe
        trailing_block = diffusion_block(trailing_input, condition_activation, modulation_weight[1], query_key_value_weight[1], projection_weight[1], expand_weight[1], contract_weight[1], stacked_biases[1])
        return (trailing_block, leading_block)
    trailing_block, backward_fn, leading_block = jax.vjp(forward, block_input.astype(jnp.float32), label_table.astype(jnp.float32), time_table.astype(jnp.float32), jnp.zeros(block_input.shape, jnp.float32), ada_weight.astype(jnp.float32), qkv_weight.astype(jnp.float32), proj_weight.astype(jnp.float32), fc1_weight.astype(jnp.float32), fc2_weight.astype(jnp.float32), block_bias.astype(jnp.float32), has_aux=True)
    grads = backward_fn(output_cotangent.astype(jnp.float32))
    block_outputs = jnp.stack([leading_block.astype(jnp.bfloat16), trailing_block.astype(jnp.bfloat16)])
    input_grads = jnp.stack([grads[0].astype(jnp.bfloat16), grads[3].astype(jnp.bfloat16)])
    return (block_outputs, input_grads, grads[4], grads[5], grads[6], grads[7], grads[8], grads[9], grads[1], grads[2])
```

```python
import jax
import jax.numpy as jnp
from jax import lax
from jax.sharding import Mesh, PartitionSpec as P

HEADS = 16
HEAD_DIM = 72
EPS = 1e-06
BF = jnp.bfloat16
F32 = jnp.float32


def flip(value, axis, by=1):
    n = lax.axis_size(axis)
    return lax.ppermute(value, axis, [(i, i ^ by) for i in range(n)])


def bit_of(axis, by):
    return (lax.axis_index(axis) // by) % 2


def gather_small(value, axes):
    for axis in reversed(axes):
        by = 1
        while by < lax.axis_size(axis):
            other = flip(value, axis, by)
            low = bit_of(axis, by) == 0
            value = jnp.where(
                low,
                jnp.concatenate([value, other], 0),
                jnp.concatenate([other, value], 0),
            )
            by *= 2
    return value


def scatter_sum_small(value, axes):
    for axis in axes:
        by = lax.axis_size(axis) // 2
        while by >= 1:
            half = value.shape[0] // 2
            low = bit_of(axis, by) == 0
            keep = jnp.where(low, value[:half], value[half:])
            send = jnp.where(low, value[half:], value[:half])
            value = keep + flip(send, axis, by)
            by //= 2
    return value


def sum_small(value, axis):
    by = 1
    while by < lax.axis_size(axis):
        value = value + flip(value, axis, by)
        by *= 2
    return value


def pick(value, index, dim=0):
    return lax.dynamic_index_in_dim(value, index, dim, keepdims=False)


def dot(a, b, dims):
    return lax.dot_general(a, b, (dims, ((), ())), preferred_element_type=F32)


def mm(a, b):
    return dot(a, b, ((1,), (0,)))


def mm_t(a, b):
    return dot(a, b, ((1,), (1,)))


def t_mm(a, b):
    return dot(a, b, ((0,), (0,)))


def norm_rows(rows):
    centred = rows - jnp.mean(rows, axis=-1, keepdims=True)
    inverse = lax.rsqrt(jnp.mean(centred * centred, axis=-1, keepdims=True) + EPS)
    return centred * inverse, inverse


def norm_back(d_normed, normed, inverse):
    first = jnp.mean(d_normed, axis=-1, keepdims=True)
    second = jnp.mean(d_normed * normed, axis=-1, keepdims=True)
    return inverse * (d_normed - first - normed * second)


def gelu_tanh(values):
    return jax.nn.gelu(values, approximate=True)


def attention(queries, keys, vals):
    tokens, width = queries.shape
    shape = (tokens, HEADS, HEAD_DIM)
    q, k, v = (part.reshape(shape) for part in (queries, keys, vals))
    scores = jnp.einsum("shd,thd->hst", q, k, preferred_element_type=F32) * HEAD_DIM**-0.5
    probs = jax.nn.softmax(scores, axis=-1)
    att = jnp.einsum("hst,thd->shd", probs.astype(BF), v, preferred_element_type=F32)
    return att.astype(BF).reshape(tokens, width), probs


def attention_back(queries, keys, vals, probs, d_att):
    tokens, width = queries.shape
    shape = (tokens, HEADS, HEAD_DIM)
    q, k, v, d = (part.reshape(shape) for part in (queries, keys, vals, d_att))
    low = probs.astype(BF)
    d_probs = jnp.einsum("shd,thd->hst", d, v, preferred_element_type=F32)
    d_vals = jnp.einsum("hst,shd->thd", low, d, preferred_element_type=F32)
    d_scores = probs * (d_probs - jnp.sum(probs * d_probs, axis=-1, keepdims=True))
    d_scores = d_scores.astype(BF)
    scale = HEAD_DIM**-0.5
    d_q = jnp.einsum("hst,thd->shd", d_scores, k, preferred_element_type=F32) * scale
    d_k = jnp.einsum("hst,shd->thd", d_scores, q, preferred_element_type=F32) * scale
    return tuple(part.reshape(tokens, width) for part in (d_q, d_k, d_vals))


def halves(value):
    return jnp.concatenate([value, flip(value, "sx")], 0)


def joined(partial, tokens):
    return partial[:tokens] + flip(partial[tokens:].astype(BF), "sx").astype(F32)


def forward(weights, biases, mod, z):
    w_qkv, w_proj, w_fc1, w_fc2 = weights
    b_qkv, b_proj, b_fc1, b_fc2 = biases
    shift1, scale1, gate1, shift2, scale2, gate2 = mod
    tokens = z.shape[0]
    width = z.shape[1]
    n1, inv1 = norm_rows(z)
    h1 = (n1 * (1.0 + scale1) + shift1).astype(BF)
    qkv = (mm(h1, w_qkv) + b_qkv).astype(BF)
    q, k, v = (qkv[:, i * width : (i + 1) * width] for i in range(3))
    att, probs = attention(q, k, v)
    att_out = mm(att, w_proj) + b_proj
    mixed = z + gate1 * att_out
    n2, inv2 = norm_rows(mixed)
    h2 = halves((n2 * (1.0 + scale2) + shift2).astype(BF))
    pre = [mm(h2, w) + b for w, b in zip(w_fc1, b_fc1)]
    act = jnp.concatenate([gelu_tanh(p).astype(BF) for p in pre], 1)
    mlp = joined(mm(act, w_fc2), tokens) + b_fc2
    out = (mixed + gate2 * mlp).astype(BF)
    return out, (n1, inv1, h1, q, k, v, probs, att, att_out, n2, inv2, h2, pre, act, mlp)


def backward(weights, mod, saved, g):
    w_qkv, w_proj, w_fc1, w_fc2 = weights
    shift1, scale1, gate1, shift2, scale2, gate2 = mod
    n1, inv1, h1, q, k, v, probs, att, att_out, n2, inv2, h2, pre, act, mlp = saved
    tokens = g.shape[0]
    d_gate2 = jnp.sum(g * mlp, axis=0)
    d_mlp = g * gate2
    d_b_fc2 = jnp.sum(d_mlp, axis=0)
    d_mlp = halves(d_mlp.astype(BF))
    d_fc2 = t_mm(act, d_mlp).astype(BF)
    d_act = mm_t(d_mlp, w_fc2)
    part = d_act.shape[1] // len(pre)
    d_pre = [
        jax.vjp(gelu_tanh, p)[1](d_act[:, i * part : (i + 1) * part])[0] for i, p in enumerate(pre)
    ]
    d_b_fc1 = jnp.concatenate([jnp.sum(d, axis=0) for d in d_pre])
    d_pre = [d.astype(BF) for d in d_pre]
    d_fc1 = [t_mm(h2, d).astype(BF) for d in d_pre]
    d_h2 = joined(sum(mm_t(d, w) for d, w in zip(d_pre, w_fc1)), tokens)
    d_scale2 = jnp.sum(d_h2 * n2, axis=0)
    d_shift2 = jnp.sum(d_h2, axis=0)
    d_mixed = g + norm_back(d_h2 * (1.0 + scale2), n2, inv2)
    d_gate1 = jnp.sum(d_mixed * att_out, axis=0)
    d_att = d_mixed * gate1
    d_b_proj = jnp.sum(d_att, axis=0)
    d_att = d_att.astype(BF)
    d_proj = t_mm(att, d_att).astype(BF)
    d_attended = mm_t(d_att, w_proj).astype(BF)
    d_q, d_k, d_v = attention_back(q, k, v, probs, d_attended)
    d_b_q = jnp.sum(d_q, axis=0)
    d_b_v = jnp.sum(d_v, axis=0)
    d_qkv = jnp.concatenate([d_q, d_k, d_v], 1).astype(BF)
    d_qkv_w = t_mm(h1, d_qkv).astype(BF)
    d_h1 = mm_t(d_qkv, w_qkv)
    d_scale1 = jnp.sum(d_h1 * n1, axis=0)
    d_shift1 = jnp.sum(d_h1, axis=0)
    dz = d_mixed + norm_back(d_h1 * (1.0 + scale1), n1, inv1)
    d_mod = jnp.concatenate([d_shift1, d_scale1, d_gate1, d_shift2, d_scale2, d_gate2])
    return dz.astype(BF), d_mod, (d_qkv_w, d_proj, d_fc1, d_fc2), (d_b_q, d_b_v, d_b_proj, d_b_fc1, d_b_fc2)


def per_device(
    block_input,
    labels,
    timesteps,
    label_table,
    time_table,
    ada_weight,
    qkv_weight,
    proj_weight,
    fc1_weight,
    fc2_weight,
    block_bias,
    output_cotangent,
):
    core = lax.axis_index("c")
    ix = lax.axis_index("sx")
    iy = lax.axis_index("sy")
    iz = lax.axis_index("z")
    blocks = lax.axis_size("c")
    ny, nx, nz = lax.axis_size("sy"), lax.axis_size("sx"), lax.axis_size("z")
    shards = ny * nx
    shard = iy * nx + ix
    yc = ny // blocks
    own, tokens, width = block_input.shape
    rows = width // shards
    hidden = fc1_weight.shape[2]
    f_rows = hidden // shards
    classes, steps = label_table.shape[0], time_table.shape[0]

    def rows_by_core(weight):
        weight = weight[0]
        split = weight.reshape(blocks, weight.shape[0] // blocks, weight.shape[1])
        return lax.all_to_all(split, "c", 0, 0)

    qkv_rows = rows_by_core(qkv_weight)
    proj_rows = rows_by_core(proj_weight)
    fc2_rows = rows_by_core(fc2_weight)
    fc1_cols = fc1_weight[0].reshape(rows, blocks, yc, nx, f_rows)
    fc1_cols = fc1_cols.transpose(1, 3, 0, 2, 4).reshape(blocks * nx, rows, yc * f_rows)
    fc1_cols = lax.all_to_all(fc1_cols, ("c", "sx"), 0, 0)
    fc1_cols = fc1_cols.reshape(blocks, nx * rows, yc * f_rows)
    weights = []
    for b in range(blocks):
        w_qkv = lax.all_gather(qkv_rows[b], ("sy", "sx", "c"), axis=0, tiled=True)
        w_proj = lax.all_gather(proj_rows[b], ("sy", "sx", "c"), axis=0, tiled=True)
        w_fc1 = lax.all_gather(fc1_cols[b], ("c", "sy"), axis=0, tiled=True)
        w_fc1 = w_fc1.reshape(blocks, width, yc * f_rows)
        w_fc2 = lax.all_gather(fc2_rows[b], ("sy", "c"), axis=0, tiled=True)
        weights.append((w_qkv, w_proj, [w_fc1[i] for i in range(blocks)], w_fc2))

    bias = gather_small(block_bias, ("c", "sy", "sx"))
    bias = bias.reshape(blocks, -1).astype(F32)

    every = gather_small(jnp.stack([labels, timesteps], 1), ("sy", "sx", "z"))
    label_hot = (every[:, :1] == jnp.arange(classes, dtype=jnp.int32)[None, :]).astype(BF)
    time_hot = (every[:, 1:] == jnp.arange(steps, dtype=jnp.int32)[None, :]).astype(BF)
    condition = mm(label_hot, label_table) + mm(time_hot, time_table)
    cond_low = jax.nn.silu(condition).astype(BF)
    latents = every.shape[0]
    cond_rows = pick(cond_low.reshape(latents, shards, rows), shard, 1)
    plane = pick(cond_rows.reshape(shards, nz, own, rows), iz, 1).reshape(shards * own, rows)
    mod = scatter_sum_small(mm(plane, ada_weight[0]), ("sy", "sx"))
    mod = lax.all_to_all(mod, "c", 0, 0)
    mod = mod + bias[:, : 6 * width]

    def block_biases(b):
        row = bias[b]
        zeros = jnp.zeros((width,), F32)
        b_qkv = jnp.concatenate([row[6 * width : 7 * width], zeros, row[7 * width : 8 * width]])
        b_fc1 = row[9 * width : 9 * width + hidden].reshape(blocks, yc, nx, f_rows)
        b_fc1 = pick(b_fc1, ix, 2).reshape(blocks, yc * f_rows)
        return b_qkv, row[8 * width : 9 * width], [b_fc1[i] for i in range(blocks)], row[9 * width + hidden :]

    mods = [
        tuple(mod[b, i * width : (i + 1) * width][None] for i in range(6)) for b in range(blocks)
    ]

    z = pick(block_input, core)
    outs, kept = [], []
    for b in range(blocks):
        z, saved = forward(weights[b], block_biases(b), mods[b], z.astype(F32))
        outs.append(z)
        kept.append(saved)

    g = pick(output_cotangent, core)
    in_grads, d_mods, grads, d_biases = ([None] * blocks for _ in range(4))
    for b in reversed(range(blocks)):
        g, d_mods[b], grads[b], d_biases[b] = backward(weights[b], mods[b], kept[b], g.astype(F32))
        in_grads[b] = g

    block_outputs = lax.all_to_all(jnp.stack(outs), "c", 0, 0)[None]
    input_grads = lax.all_to_all(jnp.stack(in_grads), "c", 0, 0)[None]

    qkv_g, proj_g, fc1_g, fc2_g = [], [], [], []
    for b in reversed(range(blocks)):
        d_qkv, d_proj, d_fc1, d_fc2 = grads[b]
        d_fc1 = jnp.stack(d_fc1).reshape(blocks * width, yc * f_rows)
        for out, grad, axes in (
            (fc2_g, d_fc2, ("sy", "c")),
            (fc1_g, d_fc1, ("c", "sy")),
            (proj_g, d_proj, ("sy", "sx", "c")),
            (qkv_g, d_qkv, ("sy", "sx", "c")),
        ):
            part = lax.psum_scatter(grad, axes, scatter_dimension=0, tiled=True)
            out.insert(0, lax.psum(part, "z"))

    def home(parts):
        stacked = lax.all_to_all(jnp.stack(parts), "c", 0, 0)
        return stacked.reshape(1, -1, stacked.shape[-1]).astype(F32)

    fc1_back = jnp.stack(fc1_g).reshape(blocks * nx, rows, yc * f_rows)
    fc1_back = lax.all_to_all(fc1_back, ("c", "sx"), 0, 0)
    fc1_back = fc1_back.reshape(blocks, nx, rows, yc, f_rows).transpose(2, 0, 3, 1, 4)
    fc1_back = fc1_back.reshape(1, rows, hidden).astype(F32)

    vectors = []
    for b in range(blocks):
        d_b_q, d_b_v, d_b_proj, d_b_fc1, d_b_fc2 = d_biases[b]
        here = (jnp.arange(nx) == ix)[None, :, None]
        d_b_fc1 = jnp.where(here, d_b_fc1.reshape(ny, 1, f_rows), 0.0).reshape(hidden)
        vectors.append(jnp.concatenate([d_mods[b], d_b_q, d_b_v, d_b_proj, d_b_fc1, d_b_fc2]))
    bias_sum = scatter_sum_small(jnp.concatenate(vectors), ("c", "sy", "sx"))
    bias_grad = sum_small(bias_sum, "z")[None]

    d_mod_low = lax.all_to_all(jnp.stack(d_mods).astype(BF), "c", 0, 0)
    d_mod_all = gather_small(d_mod_low, ("sy", "sx", "z"))
    ada_grad = t_mm(cond_rows, d_mod_all)[None]
    cond_here = pick(condition.reshape(latents, shards, rows), shard, 1)
    gate = jax.nn.sigmoid(cond_here)
    d_cond = mm_t(d_mod_all, ada_weight[0]) * (gate * (1.0 + cond_here * (1.0 - gate)))
    d_cond = d_cond + flip(d_cond, "c")
    d_cond = gather_small(d_cond[None], ("sy", "sx")).transpose(1, 0, 2).reshape(latents, width)
    exact = lax.Precision.HIGHEST
    label_grad = jnp.einsum("lc,ld->cd", label_hot.astype(F32), d_cond, precision=exact)
    time_grad = jnp.einsum("lc,ld->cd", time_hot.astype(F32), d_cond, precision=exact)

    return (
        block_outputs,
        input_grads,
        ada_grad,
        home(qkv_g),
        home(proj_g),
        fc1_back,
        home(fc2_g),
        bias_grad,
        label_grad,
        time_grad,
    )


def solution(mesh):
    sections, shards, replicas = (mesh.shape[name] for name in ("section", "shard", "replica"))
    nx = 2
    split = Mesh(
        mesh.devices.reshape(sections, shards // nx, nx, replicas), ("c", "sy", "sx", "z")
    )
    shard = ("sy", "sx")
    latents = ("sy", "sx", "z")
    placed = (
        P(latents, None, None),
        P(latents),
        P(latents),
        P(),
        P(),
        P("c", shard, None),
        P("c", shard, None),
        P("c", shard, None),
        P("c", shard, None),
        P("c", shard, None),
        P("c", shard),
        P(latents, None, None),
    )
    return jax.shard_map(
        per_device,
        mesh=split,
        in_specs=placed,
        out_specs=(
            P("c", latents, None, None),
            P("c", latents, None, None),
            P("c", shard, None),
            P("c", shard, None),
            P("c", shard, None),
            P("c", shard, None),
            P("c", shard, None),
            P("c", shard),
            P(),
            P(),
        ),
        check_vma=False,
    )
```
